32 devices in a mesh: dp: 16 (over z, y, x), tensor: 2 (over core).
Axes of the slice: x: 2, y: 2, z: 4, core: 2. Of those that a mesh axis runs over, the one named last changes fastest.
Arguments:
- tokens: bfloat16 [16384, 768], P('dp'), may hold values from -6 to 6
- lengths: int32 [16, 16], P('dp'), may hold values from 1 to 512, 1024 in all within a row
- w_qkv: bfloat16 [3, 768, 768], P(None, None, 'tensor'), may hold values from -0.21875 to 0.21875
- b_qv: bfloat16 [2, 768], P(None, 'tensor'), may hold values from -0.625 to 0.625
- conv_pool: bfloat16 [2, 4, 768], P(None, None, 'tensor'), may hold values from 0.049804688 to 0.59765625
- w_out: bfloat16 [768, 768], P('tensor'), may hold values from -1.25 to 1.25
- b_out: bfloat16 [768], replicated, may hold values from -0.625 to 0.625
- ln_gain: bfloat16 [2, 768], replicated, may hold values from 0.5 to 1.5
- ln_bias: bfloat16 [2, 768], replicated, may hold values from -0.625 to 0.625
- w_up: bfloat16 [768, 3072], P(None, 'tensor'), may hold values from -0.21875 to 0.21875
- b_up: bfloat16 [3072], P('tensor'), may hold values from -1.25 to 1.25
- w_down: bfloat16 [3072, 768], P('tensor'), may hold values from -0.109375 to 0.109375
- b_down: bfloat16 [768], replicated, may hold values from -0.625 to 0.625
- grad_output: bfloat16 [16384, 768], P(('dp', 'tensor')), may hold values from -6 to 6
Outputs:
- layer_output: bfloat16 [16384, 768], P(('dp', 'tensor'))
- grad_input: float32 [16384, 768], P(('dp', 'tensor'))
- grad_qkv: float32 [3, 768, 768], P(None, None, 'tensor')
- grad_qv_bias: float32 [2, 768], P(None, 'tensor')
- grad_conv: float32 [2, 4, 768], P(None, None, 'tensor')
- grad_out: float32 [768, 768], P('tensor')
- grad_out_bias: float32 [768], replicated
- grad_ln_gain: float32 [2, 768], replicated
- grad_ln_bias: float32 [2, 768], replicated
- grad_up: float32 [768, 3072], P(None, 'tensor')
- grad_up_bias: float32 [3072], P('tensor')
- grad_down: float32 [3072, 768], P('tensor')
- grad_down_bias: float32 [768], replicated
The draws below stay inside these ranges and needn't reach their ends.
Inputs may be any that keep to these rules, and one draw needn't show every extreme that they name: `lengths`: each row sums to 1024; the longest document has 512 tokens in every draw.
All inputs are finite; a program needn't handle non-finite values.
Results may differ from the reference program's by a relative error of at most 0.015.
Values may be sent and summed in bfloat16 or wider, within the bound.
No kernel may reach another device: no remote copies, remote signals or barrier semaphores. Data moves between devices by JAX's collectives and lax.ppermute only.
A program may use at most 128 MiB of HBM per device.

```python
import math
import jax
import jax.numpy as jnp
import numpy as np
from jax import lax

D = 768
HEADS = 12
HD = 64
FF = 3072
SEQ_LEN = 1024
DOCS = 16
MOST_DOC = 512
WIN = 128
SPAN = 512
STRIDE = 4
SEQS = 16
TOKENS = 16384


def levels(key, extent, pieces, smallest, top_value):
    level = 1.0
    for dim, blocks in pieces:
        heights = jax.random.uniform(jax.random.fold_in(jax.random.fold_in(key, 6), dim), (blocks,), jnp.float32, smallest / len(pieces), top_value / len(pieces))
        level = level * jnp.repeat(jnp.exp(heights), extent[dim] // blocks).reshape((-1,) + (1,) * (len(extent) - 1 - dim))
    return level


def length_profile(amount, total, limit, skew):
    weights = [(1 << 20) // math.isqrt(grade ** skew) + 1 for grade in range(2, amount + 1)]
    rest, holding = total - limit - (amount - 1), [1] * (amount - 1)
    while rest > 0:
        movable = [i for i in range(amount - 1) if holding[i] < limit]
        whole, left = sum([weights[i] for i in movable]), rest
        for i in movable:
            extra = min(limit - holding[i], max(1, left * weights[i] // whole), rest)
            holding[i] = holding[i] + extra
            rest = rest - extra
    return np.array([limit] + holding)


def uneven(rng, amount, total, reach, skew):
    if amount == 2:
        one = jax.random.randint(rng, (), max(1, total - reach), min(reach, total - 1) + 1)
        return jnp.stack([one, total - one])
    tallies = jnp.asarray(length_profile(amount, total, reach, skew), jnp.int32)
    couples = (amount - 1) // 2
    giver, taker = tallies[1:1 + 2 * couples:2], tallies[2:2 + 2 * couples:2]
    margin = jnp.minimum(giver - 1, reach - taker)
    moved = jax.random.randint(jax.random.fold_in(rng, 1), (couples,), 0, 1 << 20) % (margin + 1)
    tallies = tallies.at[1:1 + 2 * couples:2].set(giver - moved).at[2:2 + 2 * couples:2].set(taker + moved)
    return tallies[jax.random.permutation(jax.random.fold_in(rng, 2), amount)]


def bell_draw(own_key, dims, width, reach, split=(), held_as=jnp.bfloat16):
    result = jax.random.normal(own_key, dims, jnp.float32) * width
    if len(split) > 0:
        result = levels(own_key, dims, split, -0.22, 0.18) * result
    return jnp.clip(result, min=-reach, max=reach).astype(held_as)


def setup_inputs(seed: int = 0) -> dict:
    key_list = jax.random.split(jax.random.key(seed), 15)
    return {
        "tokens": bell_draw(key_list[0], (TOKENS, D), 1.0, 6.0, ((0, 16),)),
        "lengths": jax.vmap(lambda own: uneven(own, DOCS, SEQ_LEN, MOST_DOC, 2))(jax.random.split(key_list[1], SEQS)).reshape((SEQS, DOCS)).astype(jnp.int32),
        "w_qkv": bell_draw(key_list[2], (3, D, D), D ** -0.5, 0.21875, ((2, 2),)),
        "b_qv": bell_draw(key_list[3], (2, D), 0.1, 0.625, ((1, 2),)),
        "conv_pool": jnp.clip(0.049804688 + 0.54785156 * jax.random.uniform(key_list[4], (2, STRIDE, D), jnp.float32) ** levels(key_list[4], (2, STRIDE, D), ((2, 2),), -0.2, 0.2), 0.049804688, 0.59765625).astype(jnp.bfloat16),
        "w_out": bell_draw(key_list[5], (D, D), (D // 32) ** -0.5, 1.25, ((0, 2),)),
        "b_out": bell_draw(key_list[6], (D,), 0.1, 0.625),
        "ln_gain": jnp.clip(1.0 + 0.1 * jax.random.normal(key_list[7], (2, D), jnp.float32), 0.5, 1.5).astype(jnp.bfloat16),
        "ln_bias": bell_draw(key_list[8], (2, D), 0.1, 0.625),
        "w_up": bell_draw(key_list[9], (D, FF), D ** -0.5, 0.21875, ((1, 2),)),
        "b_up": bell_draw(key_list[10], (FF,), 0.2, 1.25, ((0, 2),)),
        "w_down": bell_draw(key_list[11], (FF, D), FF ** -0.5, 0.109375, ((0, 2),)),
        "b_down": bell_draw(key_list[12], (D,), 0.1, 0.625),
        "grad_output": bell_draw(key_list[13], (TOKENS, D), 1.0, 6.0, ((0, 32),)),
    }


PRECISION = lax.Precision.HIGHEST
EPSILON = 1e-05
MASKED = -1e+30

@jax.custom_vjp
def low(v):
    return lax.optimization_barrier(v.astype(jnp.bfloat16)).astype(jnp.float32)

@jax.custom_vjp
def low_back(v):
    return v

def low_keep(v):
    return (low(v), None)

def low_pass(kept, grad):
    return (grad,)

def back_keep(v):
    return (v, None)

def back_low(kept, grad):
    return (low(grad),)
low.defvjp(low_keep, low_pass)
low_back.defvjp(back_keep, back_low)

def document_ids(lengths):
    bounds = jnp.cumsum(lengths, axis=-1)
    places = jnp.arange(SEQ_LEN, dtype=jnp.int32)
    return lax.optimization_barrier(jnp.sum((places[None, :, None] >= bounds[:, None, :]).astype(jnp.int32), axis=-1))

def attention_masks(doc_ids):
    places = jnp.arange(SEQ_LEN, dtype=jnp.int32)
    relative = places[None, :] - places[:, None]
    same_doc = doc_ids[None, :] == doc_ids[:, None]
    near_mask = (relative >= -(WIN // 2)) & (relative < WIN // 2) & same_doc
    pool_places = jnp.arange(SEQ_LEN // STRIDE, dtype=jnp.int32)
    pool_rel = pool_places[None, :] - (places // STRIDE)[:, None]
    pool_reach = SPAN // (2 * STRIDE)
    first_doc = doc_ids[0::STRIDE]
    last_doc = doc_ids[STRIDE - 1::STRIDE]
    far_mask = (pool_rel >= -pool_reach) & (pool_rel < pool_reach) & (first_doc[None, :] == doc_ids[:, None]) & (last_doc[None, :] == doc_ids[:, None])
    return jnp.concatenate([near_mask, far_mask], axis=1)

def attend(sequence):
    queries, key_rows, value_rows, pool_keys, pool_values, doc_ids = sequence
    pooled = SEQ_LEN // STRIDE
    query_heads = queries.reshape(SEQ_LEN, HEADS, HD)
    all_keys = jnp.concatenate([key_rows, pool_keys], axis=0).reshape(SEQ_LEN + pooled, HEADS, HD)
    all_values = jnp.concatenate([value_rows, pool_values], axis=0).reshape(SEQ_LEN + pooled, HEADS, HD)
    scores = low_back(jnp.einsum('qhe,khe->hqk', query_heads, all_keys, precision=PRECISION) * HD ** (-0.5))
    scores = jnp.where(attention_masks(doc_ids)[None], scores, MASKED)
    row_max = lax.optimization_barrier(jnp.max(scores, axis=-1, keepdims=True))
    weights = jnp.exp(scores - row_max)
    probabilities = low(weights / lax.optimization_barrier(jnp.sum(weights, axis=-1, keepdims=True)))
    mixture = jnp.einsum('hqk,khe->qhe', probabilities, all_values, precision=PRECISION)
    return mixture.reshape(SEQ_LEN, D)

def layer_norm(values, gain_row, shift_row):
    centre = lax.optimization_barrier(jnp.mean(values, axis=-1, keepdims=True))
    centred = values - centre
    inv_scale = lax.rsqrt(lax.optimization_barrier(jnp.mean(centred * centred, axis=-1, keepdims=True)) + EPSILON)
    return centred * inv_scale * gain_row + shift_row

def layer(inputs, params, doc_ids):
    w_qkv, b_qv, conv_pool, w_out, b_out, ln_gain, ln_bias, w_up, b_up, w_down, b_down = params
    group_size = inputs.shape[0]
    pooled = SEQ_LEN // STRIDE
    flat_rows = inputs.reshape(group_size * SEQ_LEN, D)
    queries = low(low_back(jnp.dot(flat_rows, w_qkv[0], precision=PRECISION) + b_qv[0]))
    key_rows = low(low_back(jnp.dot(flat_rows, w_qkv[1], precision=PRECISION)))
    value_rows = low(low_back(jnp.dot(flat_rows, w_qkv[2], precision=PRECISION) + b_qv[1]))
    key_groups = key_rows.reshape(group_size, pooled, STRIDE, D)
    value_groups = value_rows.reshape(group_size, pooled, STRIDE, D)
    pool_keys = low(low_back(lax.optimization_barrier(jnp.sum(key_groups * conv_pool[0], axis=2))))
    pool_values = low(low_back(lax.optimization_barrier(jnp.sum(value_groups * conv_pool[1], axis=2))))
    mixture = lax.map(jax.checkpoint(attend), (queries.reshape(group_size, SEQ_LEN, D), key_rows.reshape(group_size, SEQ_LEN, D), value_rows.reshape(group_size, SEQ_LEN, D), pool_keys, pool_values, doc_ids))
    attended = low(low_back(mixture.reshape(group_size * SEQ_LEN, D)))
    branch_attn = low_back(jnp.dot(attended, w_out, precision=PRECISION))
    normed = layer_norm(flat_rows + branch_attn + b_out, ln_gain[0], ln_bias[0])
    hidden = low_back(jnp.dot(low(normed), w_up, precision=PRECISION) + b_up)
    gated_low = low(jax.nn.gelu(hidden, approximate=False))
    branch_ffn = low_back(jnp.dot(gated_low, w_down, precision=PRECISION))
    summed = normed + branch_ffn + b_down
    return layer_norm(summed, ln_gain[1], ln_bias[1]).reshape(group_size, SEQ_LEN, D)

def reference(tokens, lengths, w_qkv, b_qv, conv_pool, w_out, b_out, ln_gain, ln_bias, w_up, b_up, w_down, b_down, grad_output):
    params = tuple((array.astype(jnp.float32) for array in (w_qkv, b_qv, conv_pool, w_out, b_out, ln_gain, ln_bias, w_up, b_up, w_down, b_down)))
    doc_ids = document_ids(lengths)
    group_size = 4 if SEQS % 4 == 0 else 1
    group_count = SEQS // group_size
    inputs = tokens.astype(jnp.float32).reshape(group_count, group_size, SEQ_LEN, D)
    cotangent = grad_output.astype(jnp.float32).reshape(group_count, group_size, SEQ_LEN, D)
    doc_groups = doc_ids.reshape(group_count, group_size, SEQ_LEN)

    def one_group(totals, batch):
        group_inputs, group_cotangent, group_docs = batch
        outcome, pullback = jax.vjp(lambda first, second: layer(first, second, group_docs), group_inputs, params)
        grad_inputs, grad_params = pullback(group_cotangent)
        return (jax.tree.map(jnp.add, totals, grad_params), (outcome, grad_inputs))
    initial = jax.tree.map(jnp.zeros_like, params)
    totals, (outcome, grad_inputs) = lax.scan(one_group, initial, (inputs, cotangent, doc_groups))
    grad_qkv, grad_qv_bias, grad_conv, grad_out, grad_out_bias, grad_ln_gain, grad_ln_bias, grad_up, grad_up_bias, grad_down, grad_down_bias = totals
    return (outcome.reshape(TOKENS, D).astype(jnp.bfloat16), grad_inputs.reshape(TOKENS, D), grad_qkv, grad_qv_bias, grad_conv, grad_out, grad_out_bias, grad_ln_gain, grad_ln_bias, grad_up, grad_up_bias, grad_down, grad_down_bias)
```

```python
from functools import partial

import jax
import jax.numpy as jnp
from jax import lax
from jax.experimental import pallas as pl
from jax.experimental.pallas import tpu as pltpu
from jax.sharding import PartitionSpec as P

HD = 64
SEQ_LEN = 1024
WIN = 128
SPAN = 512
STRIDE = 4

EPSILON = 1e-05
MASKED = -1e30
F32 = jnp.float32
BF16 = jnp.bfloat16

ROWS = 128
HALF_WIN = WIN // 2
REACH = SPAN // (2 * STRIDE)
POOLED = SEQ_LEN // STRIDE
NEAR = ROWS + WIN
FAR = ROWS // STRIDE + 2 * REACH
BLOCKS = SEQ_LEN // ROWS
PAIR = 2 * HD


def dot(a, b, contract=((1,), (0,))):
    return lax.dot_general(a, b, (contract, ((), ())), preferred_element_type=F32)


def pair_rows(block):
    lane = lax.broadcasted_iota(jnp.int32, block.shape, 1)
    zero = jnp.zeros_like(block)
    return jnp.concatenate(
        [jnp.where(lane < HD, block, zero), jnp.where(lane < HD, zero, block)], axis=0
    )


def pair_merge(grid):
    merged = jnp.concatenate([grid[:HD, :ROWS], grid[HD:, ROWS:]], axis=0)
    return merged.T


def attend_forward_kernel(
    len_ref, tok_ref, w_ref, b_ref, conv_ref,
    q_ref, k_ref, v_ref, pk_ref, pv_ref, near_ref, far_ref, att_ref,
    kf_ref, vf_ref,
):
    block = pl.program_id(0)
    width = q_ref.shape[1]

    @pl.when(block == 0)
    def _():
        bias = b_ref[...].astype(F32)
        chunk = 256
        for part in range(SEQ_LEN // chunk):
            rows = pl.ds(part * chunk, chunk)
            padded = pl.ds(HALF_WIN + part * chunk, chunk)
            x = tok_ref[rows, :]
            q_ref[rows, :] = (dot(x, w_ref[0]) + bias[0:1]).astype(BF16)
            key = dot(x, w_ref[1]).astype(BF16)
            k_ref[padded, :] = key
            key = key.astype(F32)
            value = (dot(x, w_ref[2]) + bias[1:2]).astype(BF16)
            v_ref[padded, :] = value
            value = value.astype(F32)
            for c in range(width // 128):
                kf_ref[c, rows, :] = key[:, c * 128 : (c + 1) * 128]
                vf_ref[c, rows, :] = value[:, c * 128 : (c + 1) * 128]
        for ref in (k_ref, v_ref):
            ref[0:HALF_WIN, :] = jnp.zeros((HALF_WIN, width), BF16)
            ref[HALF_WIN + SEQ_LEN :, :] = jnp.zeros((HALF_WIN, width), BF16)
        conv = conv_ref[...].astype(F32)
        for which, (src, ref) in enumerate(((kf_ref, pk_ref), (vf_ref, pv_ref))):
            ref[0:REACH, :] = jnp.zeros((REACH, width), BF16)
            ref[REACH + POOLED :, :] = jnp.zeros((REACH, width), BF16)
            for c in range(width // 128):
                cols = slice(c * 128, (c + 1) * 128)
                total = jnp.zeros((POOLED, 128), F32)
                for r in range(STRIDE):
                    total = total + conv[which, r : r + 1, cols] * src[c, pl.ds(r, POOLED, stride=STRIDE), :]
                ref[REACH : REACH + POOLED, cols] = total.astype(BF16)

    start = pl.multiple_of(block * ROWS, ROWS)
    pos = start + lax.broadcasted_iota(jnp.int32, (1, ROWS), 1)
    first = jnp.zeros((1, ROWS), jnp.int32)
    last = jnp.full((1, ROWS), SEQ_LEN, jnp.int32)
    bound = jnp.int32(0)
    for d in range(len_ref.shape[1]):
        bound = bound + len_ref[0, d]
        first = jnp.where(pos >= bound, bound, first)
        last = jnp.where(pos < bound, jnp.minimum(last, bound), last)
    near_pos = start - HALF_WIN + lax.broadcasted_iota(jnp.int32, (NEAR, ROWS), 0)
    near_ok = (near_pos >= jnp.maximum(first, pos - HALF_WIN)) & (
        near_pos < jnp.minimum(last, pos + HALF_WIN)
    )
    group = pos >> 2
    far_pos = (start >> 2) - REACH + lax.broadcasted_iota(jnp.int32, (FAR, ROWS), 0)
    far_ok = (far_pos >= jnp.maximum((first + STRIDE - 1) >> 2, group - REACH)) & (
        far_pos < jnp.minimum(last >> 2, group + REACH)
    )
    near_bias = jnp.where(near_ok, 0.0, MASKED).astype(F32)
    far_bias = jnp.where(far_ok, 0.0, MASKED).astype(F32)
    near_bias = jnp.concatenate([near_bias, near_bias], axis=1)
    far_bias = jnp.concatenate([far_bias, far_bias], axis=1)
    near_rows = pl.ds(start, NEAR)
    far_rows = pl.ds(pl.multiple_of(block * (ROWS // STRIDE), ROWS // STRIDE), FAR)
    for p in range(width // PAIR):
        cols = slice(p * PAIR, (p + 1) * PAIR)
        q = pair_rows(q_ref[pl.ds(start, ROWS), cols] * jnp.asarray(HD**-0.5, BF16))
        near = dot(k_ref[near_rows, cols], q, ((1,), (1,))) + near_bias
        far = dot(pk_ref[far_rows, cols], q, ((1,), (1,))) + far_bias
        top = jnp.maximum(
            jnp.max(near, axis=0, keepdims=True), jnp.max(far, axis=0, keepdims=True)
        )
        near = jnp.exp(near - top)
        far = jnp.exp(far - top)
        total = jnp.sum(near, axis=0, keepdims=True) + jnp.sum(far, axis=0, keepdims=True)
        inverse = 1.0 / total
        near = (near * inverse).astype(BF16)
        far = (far * inverse).astype(BF16)
        near_ref[0, p] = near
        far_ref[0, p] = far
        mixed = dot(v_ref[near_rows, cols], near, ((0,), (0,)))
        mixed = mixed + dot(pv_ref[far_rows, cols], far, ((0,), (0,)))
        att_ref[:, cols] = pair_merge(mixed).astype(BF16)


def attend_backward_kernel(
    q_ref, k_ref, v_ref, pk_ref, pv_ref, near_ref, far_ref, grad_ref, conv_ref,
    out_ref, gconv_ref, gbias_ref,
    dk_ref, dv_ref, dpk_ref, dpv_ref, src_ref,
):
    block = pl.program_id(0)
    width = q_ref.shape[1]
    pairs = width // PAIR

    @pl.when(block == 0)
    def _():
        for ref in (dk_ref, dv_ref, dpk_ref, dpv_ref):
            ref[...] = jnp.zeros_like(ref)
        gbias_ref[...] = jnp.zeros_like(gbias_ref)

    start = pl.multiple_of(block * ROWS, ROWS)
    near_rows = pl.ds(start, NEAR)
    far_rows = pl.ds(pl.multiple_of(block * (ROWS // STRIDE), ROWS // STRIDE), FAR)
    scale = jnp.asarray(HD**-0.5, BF16)
    for p in range(pairs):
        cols = slice(p * PAIR, (p + 1) * PAIR)
        q = pair_rows(q_ref[pl.ds(start, ROWS), cols] * scale)
        g = pair_rows(grad_ref[pl.ds(start, ROWS), cols])
        near_low = near_ref[0, p]
        far_low = far_ref[0, p]
        near_prob = near_low.astype(F32)
        far_prob = far_low.astype(F32)
        near_k = k_ref[near_rows, cols]
        far_k = pk_ref[far_rows, cols]
        near_grad = dot(v_ref[near_rows, cols], g, ((1,), (1,)))
        far_grad = dot(pv_ref[far_rows, cols], g, ((1,), (1,)))
        delta = jnp.sum(near_prob * near_grad, axis=0, keepdims=True) + jnp.sum(
            far_prob * far_grad, axis=0, keepdims=True
        )
        near_ds = (near_prob * (near_grad - delta)).astype(BF16)
        far_ds = (far_prob * (far_grad - delta)).astype(BF16)
        grad_q = dot(near_k, near_ds, ((0,), (0,))) + dot(far_k, far_ds, ((0,), (0,)))
        grad_q = (pair_merge(grad_q) * (HD**-0.5)).astype(BF16)
        out_ref[0, pl.ds(start, ROWS), cols] = grad_q
        gbias_ref[0:1, cols] += jnp.sum(grad_q.astype(F32), axis=0, keepdims=True)
        dk_ref[p, near_rows, :] += dot(near_ds, q)
        dv_ref[p, near_rows, :] += dot(near_low, g)
        dpk_ref[p, far_rows, :] += dot(far_ds, q)
        dpv_ref[p, far_rows, :] += dot(far_low, g)

    @pl.when(block == pl.num_programs(0) - 1)
    def _():
        conv = conv_ref[...].astype(F32)
        body = pl.ds(HALF_WIN, SEQ_LEN)
        for which, (raw, dense, pooled) in enumerate(
            ((k_ref, dk_ref, dpk_ref), (v_ref, dv_ref, dpv_ref))
        ):
            for p in range(pairs):
                cols = slice(p * PAIR, (p + 1) * PAIR)
                src_ref[...] = raw[body, cols].astype(F32)
                low = pooled[p, REACH : REACH + POOLED, :].astype(BF16).astype(F32)
                for r in range(STRIDE):
                    picked = src_ref[pl.ds(r, POOLED, stride=STRIDE), :]
                    gconv_ref[which, r : r + 1, cols] = jnp.sum(low * picked, axis=0, keepdims=True)
                    strided = pl.ds(HALF_WIN + r, POOLED, stride=STRIDE)
                    dense[p, strided, :] = dense[p, strided, :] + conv[which, r : r + 1, cols] * low
                full = dense[p, body, :].astype(BF16)
                out_ref[1 + which, :, cols] = full
                if which == 1:
                    gbias_ref[1:2, cols] = jnp.sum(full.astype(F32), axis=0, keepdims=True)


def whole():
    return pl.BlockSpec(memory_space=pltpu.VMEM)


def attend_forward(tokens, lengths, w_qkv, b_qv, conv_pool):
    width = w_qkv.shape[2]
    pairs = width // PAIR
    sds = jax.ShapeDtypeStruct
    by_block = lambda i: (i, 0, 0, 0)
    return pl.pallas_call(
        attend_forward_kernel,
        grid=(BLOCKS,),
        in_specs=[pl.BlockSpec(memory_space=pltpu.SMEM), whole(), whole(), whole(), whole()],
        out_specs=[whole()] * 5
        + [
            pl.BlockSpec((1, pairs, NEAR, 2 * ROWS), by_block),
            pl.BlockSpec((1, pairs, FAR, 2 * ROWS), by_block),
            pl.BlockSpec((ROWS, width), lambda i: (i, 0)),
        ],
        out_shape=[
            sds((SEQ_LEN, width), BF16),
            sds((SEQ_LEN + WIN, width), BF16),
            sds((SEQ_LEN + WIN, width), BF16),
            sds((POOLED + 2 * REACH, width), BF16),
            sds((POOLED + 2 * REACH, width), BF16),
            sds((BLOCKS, pairs, NEAR, 2 * ROWS), BF16),
            sds((BLOCKS, pairs, FAR, 2 * ROWS), BF16),
            sds((SEQ_LEN, width), BF16),
        ],
        scratch_shapes=[pltpu.VMEM((pairs, SEQ_LEN, PAIR), F32)] * 2,
        name="attend_forward",
    )(lengths, tokens, w_qkv, b_qv, conv_pool)


def attend_backward(saved, grad_attended, conv_pool):
    queries, keys, values, pool_keys, pool_values, near, far = saved
    width = queries.shape[1]
    pairs = width // PAIR
    sds = jax.ShapeDtypeStruct
    by_block = lambda i: (i, 0, 0, 0)
    return pl.pallas_call(
        attend_backward_kernel,
        grid=(BLOCKS,),
        in_specs=[whole()] * 5
        + [
            pl.BlockSpec((1, pairs, NEAR, 2 * ROWS), by_block),
            pl.BlockSpec((1, pairs, FAR, 2 * ROWS), by_block),
            whole(),
            whole(),
        ],
        out_specs=[whole()] * 3,
        out_shape=[
            sds((3, SEQ_LEN, width), BF16),
            sds((2, STRIDE, width), F32),
            sds((2, width), F32),
        ],
        scratch_shapes=[
            pltpu.VMEM((pairs, SEQ_LEN + WIN, PAIR), F32),
            pltpu.VMEM((pairs, SEQ_LEN + WIN, PAIR), F32),
            pltpu.VMEM((pairs, POOLED + 2 * REACH, PAIR), F32),
            pltpu.VMEM((pairs, POOLED + 2 * REACH, PAIR), F32),
            pltpu.VMEM((SEQ_LEN, PAIR), F32),
        ],
        name="attend_backward",
    )(queries, keys, values, pool_keys, pool_values, near, far, grad_attended, conv_pool)


def layer_norm(values, gain_row, shift_row):
    centre = jnp.mean(values, axis=-1, keepdims=True)
    centred = values - centre
    inv_scale = lax.rsqrt(jnp.mean(centred * centred, axis=-1, keepdims=True) + EPSILON)
    normal_part = centred * inv_scale
    return (normal_part * gain_row + shift_row, normal_part, inv_scale)


def norm_backward(grad_rows, normal_part, inv_scale, gain_row):
    scaled = grad_rows * gain_row
    return inv_scale * (
        scaled
        - jnp.mean(scaled, axis=-1, keepdims=True)
        - normal_part * jnp.mean(scaled * normal_part, axis=-1, keepdims=True)
    )


def swap(values):
    return lax.ppermute(values, "tensor", [(0, 1), (1, 0)])


def bit_orders(count):
    bits = count.bit_length() - 1
    high = -(-bits // 3)
    mid = (bits - high + 1) // 2
    low = bits - high - mid
    x = tuple(range(low))
    y = tuple(range(low, low + mid))
    z = tuple(range(low + mid, bits))
    return (x + y + z, y + x + z, z[:1] + y + z[1:] + x, x + z[:1] + y + z[1:])


def exchange(values, count, bit):
    return lax.ppermute(values, "dp", [(i, i ^ (1 << bit)) for i in range(count)])


def sum_over_dp(parts):
    count = lax.axis_size("dp")
    index = lax.axis_index("dp")
    orders = bit_orders(count)
    orders = [orders[k % len(orders)] for k in range(len(parts))]
    steps = len(orders[0])
    held = list(parts)
    for s in range(steps):
        for k in range(len(held)):
            bit = orders[k][s]
            mine = (index >> bit) & 1
            half = held[k].shape[0] // 2
            send = lax.dynamic_slice_in_dim(held[k], (1 - mine) * half, half, 0)
            keep = lax.dynamic_slice_in_dim(held[k], mine * half, half, 0)
            got = exchange(send, count, bit)
            held[k] = (keep.astype(F32) + got.astype(F32)).astype(BF16)
    for s in reversed(range(steps)):
        for k in range(len(held)):
            bit = orders[k][s]
            mine = (index >> bit) & 1
            got = exchange(held[k], count, bit)
            held[k] = jnp.where(
                mine == 1,
                jnp.concatenate([got, held[k]], axis=0),
                jnp.concatenate([held[k], got], axis=0),
            )
    return held


def sum_small(values):
    count = lax.axis_size("dp")
    for bit in range(count.bit_length() - 1):
        values = values + exchange(values, count, bit)
    return values


def per_device(
    tokens, lengths, w_qkv, b_qv, conv_pool, w_out, b_out, ln_gain, ln_bias,
    w_up, b_up, w_down, b_down, grad_output,
):
    member = lax.axis_index("tensor")
    token_count, model = tokens.shape
    seq_count = lengths.shape[0]
    half_rows = token_count // 2
    own = member * half_rows
    other = (1 - member) * half_rows
    width = w_qkv.shape[2]
    units = w_up.shape[1]

    def rows_of(array, at):
        return lax.dynamic_slice_in_dim(array, at, half_rows, 0)

    def in_order(mine, theirs):
        return jnp.where(
            member == 0,
            jnp.concatenate([mine, theirs], axis=0),
            jnp.concatenate([theirs, mine], axis=0),
        )

    forward = [
        attend_forward(
            tokens[s * SEQ_LEN : (s + 1) * SEQ_LEN], lengths[s : s + 1], w_qkv, b_qv, conv_pool
        )
        for s in range(seq_count)
    ]
    attended = jnp.concatenate([f[7] for f in forward], axis=0) if seq_count > 1 else forward[0][7]

    out_send = dot(rows_of(attended, other), w_out).astype(BF16)
    out_got = swap(out_send)
    out_own = dot(rows_of(attended, own), w_out)
    gains = ln_gain.astype(F32)
    shifts = ln_bias.astype(F32)
    normed, normed_hat, normed_scale = layer_norm(
        rows_of(tokens, own).astype(F32) + out_own + out_got.astype(F32) + b_out.astype(F32),
        gains[0],
        shifts[0],
    )
    normed_low = normed.astype(BF16)
    normed_got = swap(normed_low)

    def feed(rows):
        hidden = dot(rows, w_up) + b_up.astype(F32)
        phi = 0.5 * lax.erfc(hidden * (-(0.5**0.5)))
        slope = phi + hidden * (jnp.exp(-0.5 * hidden * hidden) * 0.3989422804014327)
        return (hidden * phi).astype(BF16), slope.astype(BF16)

    gated_own, slope_own = feed(normed_low)
    gated_other, slope_other = feed(normed_got)
    down_got = swap(dot(gated_other, w_down).astype(BF16))
    down_own = dot(gated_own, w_down)
    output_full, output_hat, output_scale = layer_norm(
        normed + down_own + down_got.astype(F32) + b_down.astype(F32), gains[1], shifts[1]
    )
    layer_output = output_full.astype(BF16)
    grad_top = grad_output.astype(F32)
    grad_summed = norm_backward(grad_top, output_hat, output_scale, gains[1])
    gain_top = jnp.sum(grad_top * output_hat, axis=0)
    shift_top = jnp.sum(grad_top, axis=0)
    down_bias = jnp.sum(grad_summed, axis=0)
    summed_low = grad_summed.astype(BF16)
    summed_got = swap(summed_low)

    def back(rows, slope):
        return (dot(rows, w_down, ((1,), (1,))) * slope.astype(F32)).astype(BF16)

    hidden_own = back(summed_low, slope_own)
    hidden_other = back(summed_got, slope_other)
    up_got = swap(dot(hidden_other, w_up, ((1,), (1,))).astype(BF16))
    up_own = dot(hidden_own, w_up, ((1,), (1,)))
    gated_all = jnp.concatenate([gated_own, gated_other], axis=0)
    summed_all = jnp.concatenate([summed_low, summed_got], axis=0)
    hidden_all = jnp.concatenate([hidden_own, hidden_other], axis=0)
    normed_all = jnp.concatenate([normed_low, normed_got], axis=0)
    grad_down = dot(gated_all, summed_all, ((0,), (0,))).astype(BF16)
    grad_up = dot(normed_all, hidden_all, ((0,), (0,))).astype(BF16)
    up_bias = jnp.sum(hidden_all.astype(F32), axis=0)
    feed_parts = [
        grad_down[: units // 2],
        grad_down[units // 2 :],
        grad_up[:, : units // 2],
        grad_up[:, units // 2 :],
    ]
    feed_parts = sum_over_dp(feed_parts)

    grad_normed = grad_summed + up_own + up_got.astype(F32)
    grad_pre = norm_backward(grad_normed, normed_hat, normed_scale, gains[0])
    gain_first = jnp.sum(grad_normed * normed_hat, axis=0)
    shift_first = jnp.sum(grad_normed, axis=0)
    out_bias = jnp.sum(grad_pre, axis=0)
    pre_low = grad_pre.astype(BF16)
    pre_all = in_order(pre_low, swap(pre_low))
    grad_attended = dot(pre_all, w_out, ((1,), (1,))).astype(BF16)
    grad_out = dot(attended, pre_all, ((0,), (0,))).astype(BF16)
    backward = [
        attend_backward(
            forward[s][:7], grad_attended[s * SEQ_LEN : (s + 1) * SEQ_LEN], conv_pool
        )
        for s in range(seq_count)
    ]
    if seq_count > 1:
        grad_qkv_low = jnp.concatenate([b[0] for b in backward], axis=1)
    else:
        grad_qkv_low = backward[0][0]
    grad_conv = sum(b[1] for b in backward)
    grad_qv_bias = sum(b[2] for b in backward)
    attn_parts = [dot(tokens, grad_qkv_low[k], ((0,), (0,))).astype(BF16) for k in range(3)]
    attn_parts.append(jnp.concatenate([grad_out[:, : model // 2], grad_out[:, model // 2 :]], axis=0))
    attn_parts = sum_over_dp(attn_parts)

    def input_rows(at):
        return sum(
            dot(rows_of(grad_qkv_low[k], at), w_qkv[k], ((1,), (1,))) for k in range(3)
        )

    input_got = swap(input_rows(other).astype(BF16))
    grad_input = grad_pre + input_rows(own) + input_got.astype(F32)

    norm_rows = jnp.concatenate(
        [out_bias, gain_first, gain_top, shift_first, shift_top, down_bias], axis=0
    )
    norm_rows = norm_rows + swap(norm_rows)
    small = jnp.concatenate(
        [norm_rows, grad_qv_bias.reshape(-1), grad_conv.reshape(-1), up_bias], axis=0
    )
    size = small.shape[0]
    small = jnp.pad(small, (0, -size % 1024)).reshape(-1, 128)
    small = sum_small(small).reshape(-1)
    cuts = [model, 2 * model, 2 * model, model]
    places = []
    at = 0
    for cut in cuts + [2 * width, 2 * STRIDE * width, units]:
        places.append(small[at : at + cut])
        at += cut
    out_bias, gain_grad, shift_grad, down_bias, grad_qv_bias, grad_conv, up_bias = places

    grad_down = jnp.concatenate(feed_parts[:2], axis=0).astype(F32)
    grad_up = jnp.concatenate(feed_parts[2:], axis=1).astype(F32)
    grad_qkv = jnp.stack(attn_parts[:3]).astype(F32)
    grad_out = jnp.concatenate(
        [attn_parts[3][:width], attn_parts[3][width:]], axis=1
    ).astype(F32)
    return (
        layer_output,
        grad_input,
        grad_qkv,
        grad_qv_bias.reshape(2, width),
        grad_conv.reshape(2, STRIDE, width),
        grad_out,
        out_bias,
        gain_grad.reshape(2, model),
        shift_grad.reshape(2, model),
        grad_up,
        up_bias,
        grad_down,
        down_bias,
    )


def solution(mesh):
    placed = (
        P("dp", None),
        P("dp", None),
        P(None, None, "tensor"),
        P(None, "tensor"),
        P(None, None, "tensor"),
        P("tensor", None),
        P(),
        P(),
        P(),
        P(None, "tensor"),
        P("tensor"),
        P("tensor", None),
        P(),
        P(("dp", "tensor"), None),
    )
    return jax.shard_map(
        per_device,
        mesh=mesh,
        in_specs=placed,
        out_specs=(
            P(("dp", "tensor"), None),
            P(("dp", "tensor"), None),
            P(None, None, "tensor"),
            P(None, "tensor"),
            P(None, None, "tensor"),
            P("tensor", None),
            P(),
            P(),
            P(),
            P(None, "tensor"),
            P("tensor"),
            P("tensor", None),
            P(),
        ),
        check_vma=False,
    )
```

```python
from functools import partial

import jax
import jax.numpy as jnp
from jax import lax
from jax.experimental import pallas as pl
from jax.experimental.pallas import tpu as pltpu
from jax.sharding import PartitionSpec as P

HD = 64
SEQ_LEN = 1024
WIN = 128
SPAN = 512
STRIDE = 4

EPSILON = 1e-05
MASKED = -1e30
F32 = jnp.float32
BF16 = jnp.bfloat16

ROWS = 128
HALF_WIN = WIN // 2
REACH = SPAN // (2 * STRIDE)
POOLED = SEQ_LEN // STRIDE
NEAR = ROWS + WIN
FAR = ROWS // STRIDE + 2 * REACH
BLOCKS = SEQ_LEN // ROWS
PAIR = 2 * HD


NT = ((1,), (1,))
TN = ((0,), (0,))
SLABS = 16
UNITS = 256


def dot(a, b, contract=((1,), (0,))):
    return lax.dot_general(a, b, (contract, ((), ())), preferred_element_type=F32)


def pair_rows(block):
    lane = lax.broadcasted_iota(jnp.int32, block.shape, 1)
    zero = jnp.zeros_like(block)
    return jnp.concatenate(
        [jnp.where(lane < HD, block, zero), jnp.where(lane < HD, zero, block)], axis=0
    )


def pair_merge(grid):
    merged = jnp.concatenate([grid[:HD, :ROWS], grid[HD:, ROWS:]], axis=0)
    return merged.T


def attend_forward_kernel(
    at_ref, len_ref, tok_ref, w_ref, b_ref, conv_ref, wo_ref,
    q_ref, k_ref, v_ref, pk_ref, pv_ref, near_ref, far_ref, att_ref, send_ref, own_ref,
    kf_ref, vf_ref,
):
    block = pl.program_id(0)
    width = q_ref.shape[1]

    @pl.when(block == 0)
    def _():
        bias = b_ref[...].astype(F32)
        chunk = 256
        for part in range(SEQ_LEN // chunk):
            rows = pl.ds(part * chunk, chunk)
            padded = pl.ds(HALF_WIN + part * chunk, chunk)
            x = tok_ref[rows, :]
            q_ref[rows, :] = (dot(x, w_ref[0]) + bias[0:1]).astype(BF16)
            key = dot(x, w_ref[1]).astype(BF16)
            k_ref[padded, :] = key
            key = key.astype(F32)
            value = (dot(x, w_ref[2]) + bias[1:2]).astype(BF16)
            v_ref[padded, :] = value
            value = value.astype(F32)
            for c in range(width // 128):
                kf_ref[c, rows, :] = key[:, c * 128 : (c + 1) * 128]
                vf_ref[c, rows, :] = value[:, c * 128 : (c + 1) * 128]
        for ref in (k_ref, v_ref):
            ref[0:HALF_WIN, :] = jnp.zeros((HALF_WIN, width), BF16)
            ref[HALF_WIN + SEQ_LEN :, :] = jnp.zeros((HALF_WIN, width), BF16)
        conv = conv_ref[...].astype(F32)
        for which, (src, ref) in enumerate(((kf_ref, pk_ref), (vf_ref, pv_ref))):
            ref[0:REACH, :] = jnp.zeros((REACH, width), BF16)
            ref[REACH + POOLED :, :] = jnp.zeros((REACH, width), BF16)
            for c in range(width // 128):
                cols = slice(c * 128, (c + 1) * 128)
                total = jnp.zeros((POOLED, 128), F32)
                for r in range(STRIDE):
                    total = total + conv[which, r : r + 1, cols] * src[c, pl.ds(r, POOLED, stride=STRIDE), :]
                ref[REACH : REACH + POOLED, cols] = total.astype(BF16)

    start = pl.multiple_of(block * ROWS, ROWS)
    pos = start + lax.broadcasted_iota(jnp.int32, (1, ROWS), 1)
    first = jnp.zeros((1, ROWS), jnp.int32)
    last = jnp.full((1, ROWS), SEQ_LEN, jnp.int32)
    bound = jnp.int32(0)
    for d in range(len_ref.shape[1]):
        bound = bound + len_ref[0, d]
        first = jnp.where(pos >= bound, bound, first)
        last = jnp.where(pos < bound, jnp.minimum(last, bound), last)
    near_pos = start - HALF_WIN + lax.broadcasted_iota(jnp.int32, (NEAR, ROWS), 0)
    near_ok = (near_pos >= jnp.maximum(first, pos - HALF_WIN)) & (
        near_pos < jnp.minimum(last, pos + HALF_WIN)
    )
    group = pos >> 2
    far_pos = (start >> 2) - REACH + lax.broadcasted_iota(jnp.int32, (FAR, ROWS), 0)
    far_ok = (far_pos >= jnp.maximum((first + STRIDE - 1) >> 2, group - REACH)) & (
        far_pos < jnp.minimum(last >> 2, group + REACH)
    )
    near_bias = jnp.where(near_ok, 0.0, MASKED).astype(F32)
    far_bias = jnp.where(far_ok, 0.0, MASKED).astype(F32)
    near_bias = jnp.concatenate([near_bias, near_bias], axis=1)
    far_bias = jnp.concatenate([far_bias, far_bias], axis=1)
    near_rows = pl.ds(start, NEAR)
    far_rows = pl.ds(pl.multiple_of(block * (ROWS // STRIDE), ROWS // STRIDE), FAR)
    for p in range(width // PAIR):
        cols = slice(p * PAIR, (p + 1) * PAIR)
        q = pair_rows(q_ref[pl.ds(start, ROWS), cols] * jnp.asarray(HD**-0.5, BF16))
        near = dot(k_ref[near_rows, cols], q, ((1,), (1,))) + near_bias
        far = dot(pk_ref[far_rows, cols], q, ((1,), (1,))) + far_bias
        top = jnp.maximum(
            jnp.max(near, axis=0, keepdims=True), jnp.max(far, axis=0, keepdims=True)
        )
        near = jnp.exp(near - top)
        far = jnp.exp(far - top)
        total = jnp.sum(near, axis=0, keepdims=True) + jnp.sum(far, axis=0, keepdims=True)
        inverse = 1.0 / total
        near = (near * inverse).astype(BF16)
        far = (far * inverse).astype(BF16)
        near_ref[0, p] = near
        far_ref[0, p] = far
        mixed = dot(v_ref[near_rows, cols], near, ((0,), (0,)))
        mixed = mixed + dot(pv_ref[far_rows, cols], far, ((0,), (0,)))
        att_ref[pl.ds(start, ROWS), cols] = pair_merge(mixed).astype(BF16)

    @pl.when(block == pl.num_programs(0) - 1)
    def _():
        half = SEQ_LEN // 2
        own = pl.multiple_of(at_ref[0], half)
        send_ref[...] = dot(att_ref[pl.ds(half - own, half), :], wo_ref[...]).astype(BF16)
        own_ref[...] = dot(att_ref[pl.ds(own, half), :], wo_ref[...])


def attend_backward_kernel(
    at_ref, q_ref, k_ref, v_ref, pk_ref, pv_ref, near_ref, far_ref, mine_ref, theirs_ref, wo_ref, conv_ref,
    out_ref, gconv_ref, gbias_ref,
    dk_ref, dv_ref, dpk_ref, dpv_ref, src_ref, grad_ref,
):
    block = pl.program_id(0)
    width = q_ref.shape[1]
    pairs = width // PAIR

    @pl.when(block == 0)
    def _():
        for ref in (dk_ref, dv_ref, dpk_ref, dpv_ref):
            ref[...] = jnp.zeros_like(ref)
        gbias_ref[...] = jnp.zeros_like(gbias_ref)
        half = SEQ_LEN // 2
        own = pl.multiple_of(at_ref[0], half)
        grad_ref[pl.ds(own, half), :] = dot(mine_ref[...], wo_ref[...], NT).astype(BF16)
        grad_ref[pl.ds(half - own, half), :] = dot(theirs_ref[...], wo_ref[...], NT).astype(BF16)

    start = pl.multiple_of(block * ROWS, ROWS)
    near_rows = pl.ds(start, NEAR)
    far_rows = pl.ds(pl.multiple_of(block * (ROWS // STRIDE), ROWS // STRIDE), FAR)
    scale = jnp.asarray(HD**-0.5, BF16)
    for p in range(pairs):
        cols = slice(p * PAIR, (p + 1) * PAIR)
        q = pair_rows(q_ref[pl.ds(start, ROWS), cols] * scale)
        g = pair_rows(grad_ref[pl.ds(start, ROWS), cols])
        near_low = near_ref[0, p]
        far_low = far_ref[0, p]
        near_prob = near_low.astype(F32)
        far_prob = far_low.astype(F32)
        near_k = k_ref[near_rows, cols]
        far_k = pk_ref[far_rows, cols]
        near_grad = dot(v_ref[near_rows, cols], g, ((1,), (1,)))
        far_grad = dot(pv_ref[far_rows, cols], g, ((1,), (1,)))
        delta = jnp.sum(near_prob * near_grad, axis=0, keepdims=True) + jnp.sum(
            far_prob * far_grad, axis=0, keepdims=True
        )
        near_ds = (near_prob * (near_grad - delta)).astype(BF16)
        far_ds = (far_prob * (far_grad - delta)).astype(BF16)
        grad_q = dot(near_k, near_ds, ((0,), (0,))) + dot(far_k, far_ds, ((0,), (0,)))
        grad_q = (pair_merge(grad_q) * (HD**-0.5)).astype(BF16)
        out_ref[0, pl.ds(start, ROWS), cols] = grad_q
        gbias_ref[0:1, cols] += jnp.sum(grad_q.astype(F32), axis=0, keepdims=True)
        dk_ref[p, near_rows, :] += dot(near_ds, q)
        dv_ref[p, near_rows, :] += dot(near_low, g)
        dpk_ref[p, far_rows, :] += dot(far_ds, q)
        dpv_ref[p, far_rows, :] += dot(far_low, g)

    @pl.when(block == pl.num_programs(0) - 1)
    def _():
        conv = conv_ref[...].astype(F32)
        body = pl.ds(HALF_WIN, SEQ_LEN)
        for which, (raw, dense, pooled) in enumerate(
            ((k_ref, dk_ref, dpk_ref), (v_ref, dv_ref, dpv_ref))
        ):
            for p in range(pairs):
                cols = slice(p * PAIR, (p + 1) * PAIR)
                src_ref[...] = raw[body, cols].astype(F32)
                low = pooled[p, REACH : REACH + POOLED, :].astype(BF16).astype(F32)
                for r in range(STRIDE):
                    picked = src_ref[pl.ds(r, POOLED, stride=STRIDE), :]
                    gconv_ref[which, r : r + 1, cols] = jnp.sum(low * picked, axis=0, keepdims=True)
                    strided = pl.ds(HALF_WIN + r, POOLED, stride=STRIDE)
                    dense[p, strided, :] = dense[p, strided, :] + conv[which, r : r + 1, cols] * low
                full = dense[p, body, :].astype(BF16)
                out_ref[1 + which, :, cols] = full
                if which == 1:
                    gbias_ref[1:2, cols] = jnp.sum(full.astype(F32), axis=0, keepdims=True)


def whole():
    return pl.BlockSpec(memory_space=pltpu.VMEM)


def scalars():
    return pl.BlockSpec(memory_space=pltpu.SMEM)


def call(kernel, name, outs, args, grid=None, in_specs=None, out_specs=None, scratch=(), cost=None):
    sds = [jax.ShapeDtypeStruct(shape, kind) for shape, kind in outs]
    flops, moved = cost if cost else (1_000_000, 1_000_000)
    return pl.pallas_call(
        kernel,
        grid=grid if grid else (),
        in_specs=in_specs if in_specs else [whole() for _ in args],
        out_specs=out_specs if out_specs else [whole() for _ in outs],
        out_shape=sds,
        scratch_shapes=list(scratch),
        cost_estimate=pl.CostEstimate(flops=flops, bytes_accessed=moved, transcendentals=0),
        name=name,
    )(*args)


def attend_forward(at, tokens, lengths, w_qkv, b_qv, conv_pool, w_out):
    width = w_qkv.shape[2]
    model = tokens.shape[1]
    pairs = width // PAIR
    by_block = lambda i: (i, 0, 0, 0)
    half = SEQ_LEN // 2
    return call(
        attend_forward_kernel,
        "attend_forward",
        [
            ((SEQ_LEN, width), BF16),
            ((SEQ_LEN + WIN, width), BF16),
            ((SEQ_LEN + WIN, width), BF16),
            ((POOLED + 2 * REACH, width), BF16),
            ((POOLED + 2 * REACH, width), BF16),
            ((BLOCKS, pairs, NEAR, 2 * ROWS), BF16),
            ((BLOCKS, pairs, FAR, 2 * ROWS), BF16),
            ((SEQ_LEN, width), BF16),
            ((half, model), BF16),
            ((half, model), F32),
        ],
        (at, lengths, tokens, w_qkv, b_qv, conv_pool, w_out),
        grid=(BLOCKS,),
        in_specs=[scalars(), scalars()] + [whole()] * 5,
        out_specs=[whole()] * 5
        + [
            pl.BlockSpec((1, pairs, NEAR, 2 * ROWS), by_block),
            pl.BlockSpec((1, pairs, FAR, 2 * ROWS), by_block),
        ]
        + [whole()] * 3,
        scratch=[pltpu.VMEM((pairs, SEQ_LEN, PAIR), F32)] * 2,
        cost=(4_000_000_000, 16_000_000),
    )


def attend_backward(at, saved, mine, theirs, w_out, conv_pool):
    queries, keys, values, pool_keys, pool_values, near, far = saved
    width = queries.shape[1]
    pairs = width // PAIR
    by_block = lambda i: (i, 0, 0, 0)
    return call(
        attend_backward_kernel,
        "attend_backward",
        [
            ((3, SEQ_LEN, width), BF16),
            ((2, STRIDE, width), F32),
            ((2, width), F32),
        ],
        (at, queries, keys, values, pool_keys, pool_values, near, far, mine, theirs, w_out, conv_pool),
        grid=(BLOCKS,),
        in_specs=[scalars()]
        + [whole()] * 5
        + [
            pl.BlockSpec((1, pairs, NEAR, 2 * ROWS), by_block),
            pl.BlockSpec((1, pairs, FAR, 2 * ROWS), by_block),
        ]
        + [whole()] * 4,
        scratch=[
            pltpu.VMEM((pairs, SEQ_LEN + WIN, PAIR), F32),
            pltpu.VMEM((pairs, SEQ_LEN + WIN, PAIR), F32),
            pltpu.VMEM((pairs, POOLED + 2 * REACH, PAIR), F32),
            pltpu.VMEM((pairs, POOLED + 2 * REACH, PAIR), F32),
            pltpu.VMEM((SEQ_LEN, PAIR), F32),
            pltpu.VMEM((SEQ_LEN, width), BF16),
        ],
        cost=(6_000_000_000, 16_000_000),
    )


def row_mean(values):
    return jnp.sum(values, axis=1, keepdims=True) * (1.0 / values.shape[1])


def layer_norm(values, gain_row, shift_row):
    centred = values - row_mean(values)
    inv_scale = lax.rsqrt(row_mean(centred * centred) + EPSILON)
    normal_part = centred * inv_scale
    return (normal_part * gain_row + shift_row, normal_part, inv_scale)


def norm_backward(grad_rows, normal_part, inv_scale, gain_row):
    scaled = grad_rows * gain_row
    return inv_scale * (scaled - row_mean(scaled) - normal_part * row_mean(scaled * normal_part))


def column_sum(values):
    return jnp.sum(values, axis=0, keepdims=True)


CHUNK = 128


def first_norm_kernel(at_ref, tok_ref, own_ref, got_ref, bias_ref, gain_ref, shift_ref, normed_ref, low_ref, hat_ref, scale_ref):
    half = own_ref.shape[0]
    own = at_ref[0]

    def step(c, _):
        rows = pl.ds(pl.multiple_of(c * CHUNK, CHUNK), CHUNK)
        token_rows = pl.ds(pl.multiple_of(own + c * CHUNK, CHUNK), CHUNK)
        total = tok_ref[token_rows, :].astype(F32) + own_ref[rows, :] + got_ref[rows, :].astype(F32)
        total = total + bias_ref[...].astype(F32)
        normed, hat, scale = layer_norm(total, gain_ref[0:1].astype(F32), shift_ref[0:1].astype(F32))
        normed_ref[rows, :] = normed
        low_ref[rows, :] = normed.astype(BF16)
        hat_ref[rows, :] = hat.astype(BF16)
        scale_ref[rows, :] = scale
        return 0

    lax.fori_loop(0, half // CHUNK, step, 0)


def second_norm_kernel(part_ref, got_ref, gain_ref, shift_ref, grad_ref, out_ref, summed_ref, low_ref, sums_ref):
    half = part_ref.shape[0]
    gain = gain_ref[1:2].astype(F32)
    shift = shift_ref[1:2].astype(F32)
    sums_ref[...] = jnp.zeros_like(sums_ref)

    def step(c, _):
        rows = pl.ds(pl.multiple_of(c * CHUNK, CHUNK), CHUNK)
        full, hat, scale = layer_norm(part_ref[rows, :] + got_ref[rows, :].astype(F32), gain, shift)
        out_ref[rows, :] = full.astype(BF16)
        grad = grad_ref[rows, :].astype(F32)
        summed = norm_backward(grad, hat, scale, gain)
        summed_ref[rows, :] = summed
        low_ref[rows, :] = summed.astype(BF16)
        sums_ref[0:1, :] += column_sum(grad * hat)
        sums_ref[1:2, :] += column_sum(grad)
        sums_ref[2:3, :] += column_sum(summed)
        return 0

    lax.fori_loop(0, half // CHUNK, step, 0)


def first_back_kernel(part_ref, got_ref, hat_ref, scale_ref, gain_ref, pre_ref, low_ref, sums_ref):
    half = part_ref.shape[0]
    gain = gain_ref[0:1].astype(F32)
    sums_ref[...] = jnp.zeros_like(sums_ref)

    def step(c, _):
        rows = pl.ds(pl.multiple_of(c * CHUNK, CHUNK), CHUNK)
        grad = part_ref[rows, :] + got_ref[rows, :].astype(F32)
        hat = hat_ref[rows, :].astype(F32)
        pre = norm_backward(grad, hat, scale_ref[rows, :], gain)
        pre_ref[rows, :] = pre
        low_ref[rows, :] = pre.astype(BF16)
        sums_ref[0:1, :] += column_sum(grad * hat)
        sums_ref[1:2, :] += column_sum(grad)
        sums_ref[2:3, :] += column_sum(pre)
        return 0

    lax.fori_loop(0, half // CHUNK, step, 0)


TAIL_RATE = 0.30000000000000016
TAIL = (
    0.11962929504860834,
    0.12075402115242218,
    0.09991304007979376,
    0.12856326552160616,
    -0.05368700171650854,
    0.20635740430193542,
    -0.15720546626462548,
    0.035675368723835546,
)
DENSITY = 0.3989422804014327


def gelu_and_slope(hidden):
    size = jnp.abs(hidden)
    t = 1.0 / (1.0 + TAIL_RATE * size)
    bell = jnp.exp(-0.5 * hidden * hidden)
    tail = jnp.full_like(t, TAIL[-1])
    for term in TAIL[-2::-1]:
        tail = tail * t + term
    tail = tail * t * bell
    phi = jnp.where(hidden >= 0, 1.0 - tail, tail)
    return hidden * phi, phi + hidden * (bell * DENSITY)


def feed_step(rows_ref, up_ref, bias_ref, down_ref, gated_ref, slope_ref, acc_ref):
    bias = bias_ref[...].astype(F32)
    part = 128
    for c in range(rows_ref.shape[0] // part):
        rows = slice(c * part, (c + 1) * part)
        hidden = dot(rows_ref[rows, :], up_ref[...]) + bias
        gated, slope = gelu_and_slope(hidden)
        gated = gated.astype(BF16)
        gated_ref[rows, :] = gated
        slope_ref[rows, :] = slope.astype(BF16)
        acc_ref[rows, :] += dot(gated, down_ref[...])


def feed_own_kernel(rows_ref, up_ref, bias_ref, down_ref, normed_ref, after_ref, gated_ref, slope_ref, out_ref):
    @pl.when(pl.program_id(0) == 0)
    def _():
        out_ref[...] = normed_ref[...] + after_ref[...].astype(F32)

    feed_step(rows_ref, up_ref, bias_ref, down_ref, gated_ref, slope_ref, out_ref)


def feed_other_kernel(rows_ref, up_ref, bias_ref, down_ref, gated_ref, slope_ref, out_ref, acc_ref):
    @pl.when(pl.program_id(0) == 0)
    def _():
        acc_ref[...] = jnp.zeros_like(acc_ref)

    feed_step(rows_ref, up_ref, bias_ref, down_ref, gated_ref, slope_ref, acc_ref)

    @pl.when(pl.program_id(0) == pl.num_programs(0) - 1)
    def _():
        out_ref[...] = acc_ref[...].astype(BF16)


def feed(rows, w_up, b_up, w_down, normed=None, b_down=None):
    count, model = rows.shape
    units = w_up.shape[1]
    own = normed is not None
    args = [rows, w_up, b_up, w_down] + ([normed, b_down] if own else [])
    specs = [
        whole(),
        pl.BlockSpec((model, UNITS), lambda j: (0, j)),
        pl.BlockSpec((1, UNITS), lambda j: (0, j)),
        pl.BlockSpec((UNITS, model), lambda j: (j, 0)),
    ] + ([whole(), whole()] if own else [])
    block = pl.BlockSpec((count, UNITS), lambda j: (0, j))
    return call(
        feed_own_kernel if own else feed_other_kernel,
        "feed_own" if own else "feed_other",
        [((count, units), BF16), ((count, units), BF16), ((count, model), F32 if own else BF16)],
        args,
        grid=(units // UNITS,),
        in_specs=specs,
        out_specs=[block, block, whole()],
        scratch=[] if own else [pltpu.VMEM((count, model), F32)],
        cost=(5_000_000_000, 10_000_000),
    )


def back_step(rows_ref, slope_ref, down_ref, up_ref, hidden_ref, bias_ref, acc_ref):
    part = 256
    total = jnp.zeros((1, UNITS), F32)
    for c in range(rows_ref.shape[0] // part):
        rows = slice(c * part, (c + 1) * part)
        grad = dot(rows_ref[rows, :], down_ref[...], NT) * slope_ref[rows, :].astype(F32)
        grad = grad.astype(BF16)
        hidden_ref[rows, :] = grad
        total = total + column_sum(grad.astype(F32))
        acc_ref[rows, :] += dot(grad, up_ref[...], NT)
    bias_ref[...] = total


def back_own_kernel(rows_ref, slope_ref, down_ref, up_ref, summed_ref, hidden_ref, bias_ref, out_ref):
    @pl.when(pl.program_id(0) == 0)
    def _():
        out_ref[...] = summed_ref[...]

    back_step(rows_ref, slope_ref, down_ref, up_ref, hidden_ref, bias_ref, out_ref)


def back_other_kernel(rows_ref, slope_ref, down_ref, up_ref, hidden_ref, bias_ref, out_ref, acc_ref):
    @pl.when(pl.program_id(0) == 0)
    def _():
        acc_ref[...] = jnp.zeros_like(acc_ref)

    back_step(rows_ref, slope_ref, down_ref, up_ref, hidden_ref, bias_ref, acc_ref)

    @pl.when(pl.program_id(0) == pl.num_programs(0) - 1)
    def _():
        out_ref[...] = acc_ref[...].astype(BF16)


def back(rows, slope, w_down, w_up, summed=None):
    count, model = rows.shape
    units = w_up.shape[1]
    own = summed is not None
    block = pl.BlockSpec((count, UNITS), lambda j: (0, j))
    return call(
        back_own_kernel if own else back_other_kernel,
        "back_own" if own else "back_other",
        [((count, units), BF16), ((1, units), F32), ((count, model), F32 if own else BF16)],
        [rows, slope, w_down, w_up] + ([summed] if own else []),
        grid=(units // UNITS,),
        in_specs=[
            whole(),
            block,
            pl.BlockSpec((UNITS, model), lambda j: (j, 0)),
            pl.BlockSpec((model, UNITS), lambda j: (0, j)),
        ]
        + ([whole()] if own else []),
        out_specs=[block, pl.BlockSpec((1, UNITS), lambda j: (0, j)), whole()],
        scratch=[] if own else [pltpu.VMEM((count, model), F32)],
        cost=(5_000_000_000, 10_000_000),
    )


def scatter_slabs(spot, src_ref, keep_ref, send_ref):
    rows = src_ref.shape[0] // SLABS
    half = SLABS // 2

    def step(p, _):
        place = jnp.bitwise_xor(p, spot)
        value = src_ref[pl.ds(pl.multiple_of(p * rows, rows), rows), :]

        @pl.when(place < half)
        def _():
            keep_ref[place] = value

        @pl.when(place >= half)
        def _():
            send_ref[place - half] = value

        return 0

    lax.fori_loop(0, SLABS, step, 0)


def down_grad_kernel(at_ref, gated_a, gated_b, summed_a, summed_b, keep_ref, send_ref, full_ref):
    def step(j, _):
        cols = pl.ds(pl.multiple_of(j * UNITS, UNITS), UNITS)
        value = dot(gated_a[:, cols], summed_a[...], TN) + dot(gated_b[:, cols], summed_b[...], TN)
        full_ref[cols, :] = value.astype(BF16)
        return 0

    lax.fori_loop(0, full_ref.shape[0] // UNITS, step, 0)
    scatter_slabs(at_ref[1], full_ref, keep_ref, send_ref)


def up_grad_kernel(
    at_ref, gated_a, gated_b, summed_a, summed_b, normed_a, normed_b, hidden_a, hidden_b,
    keep1_ref, send1_ref, keep2_ref, send2_ref, full1_ref, full2_ref,
):
    model = normed_a.shape[1]
    value = dot(gated_a[...], summed_a[...], TN) + dot(gated_b[...], summed_b[...], TN)
    full1_ref[0:UNITS, :] = value.astype(BF16)

    def step(j, _):
        at = pl.multiple_of(j * UNITS, UNITS)
        cols = pl.ds(at, UNITS)
        left = dot(normed_a[:, cols], hidden_a[:, :model], TN) + dot(normed_b[:, cols], hidden_b[:, :model], TN)
        full1_ref[pl.ds(at + UNITS, UNITS), :] = left.astype(BF16)
        right = dot(normed_a[:, cols], hidden_a[:, model:], TN) + dot(normed_b[:, cols], hidden_b[:, model:], TN)
        full2_ref[cols, :] = right.astype(BF16)
        return 0

    lax.fori_loop(0, model // UNITS, step, 0)
    scatter_slabs(at_ref[2], full1_ref, keep1_ref, send1_ref)
    scatter_slabs(at_ref[3], full2_ref, keep2_ref, send2_ref)


def attn_grad_kernel(
    at_ref, tok_ref, grad_ref, att_ref, mine_ref, theirs_ref,
    keep0_ref, send0_ref, keep1_ref, send1_ref, keep2_ref, send2_ref, full0_ref, full1_ref, full2_ref,
):
    width = att_ref.shape[1]
    half = SEQ_LEN // 2
    own = pl.multiple_of(at_ref[0], half)

    def step(j, _):
        rows = pl.ds(pl.multiple_of(j * PAIR, PAIR), PAIR)
        upper = pl.ds(pl.multiple_of(j * PAIR + width, PAIR), PAIR)
        wide = pl.ds(pl.multiple_of(j * 2 * PAIR, 2 * PAIR), 2 * PAIR)
        x = tok_ref[:, wide]
        full0_ref[wide, :width] = dot(x, grad_ref[0], TN).astype(BF16)
        full0_ref[wide, width:] = dot(x, grad_ref[1], TN).astype(BF16)
        full1_ref[rows, :width] = dot(tok_ref[:, rows], grad_ref[2], TN).astype(BF16)
        full1_ref[rows, width:] = dot(tok_ref[:, upper], grad_ref[2], TN).astype(BF16)
        return 0

    lax.fori_loop(0, width // PAIR, step, 0)
    for c in range(width // PAIR):
        cols = slice(c * PAIR, (c + 1) * PAIR)
        value = dot(att_ref[pl.ds(own, half), cols], mine_ref[...], TN)
        value = (value + dot(att_ref[pl.ds(half - own, half), cols], theirs_ref[...], TN)).astype(BF16)
        if c == 0:
            full1_ref[width:, :] = value
        else:
            full2_ref[(c - 1) * PAIR : c * PAIR, :] = value
    scatter_slabs(at_ref[1], full0_ref, keep0_ref, send0_ref)
    scatter_slabs(at_ref[2], full1_ref, keep1_ref, send1_ref)
    scatter_slabs(at_ref[3], full2_ref, keep2_ref, send2_ref)


def slab_outs(rows, cols):
    shape = (SLABS // 2, rows // SLABS, cols)
    return [(shape, BF16), (shape, BF16)]


def slab_at(spot, held_ref, got_ref, p, write):
    place = jnp.bitwise_xor(p, spot)
    half = SLABS // 2

    @pl.when(place < half)
    def _():
        write(held_ref[place].astype(F32))

    @pl.when(place >= half)
    def _():
        write(got_ref[place - half].astype(F32))


def each_slab(spot, held_ref, got_ref, begin, end, write):
    rows = held_ref.shape[1]

    def step(p, _):
        slab_at(spot, held_ref, got_ref, p, partial(write, pl.multiple_of((p - begin) * rows, rows)))
        return 0

    lax.fori_loop(begin, end, step, 0)


def feed_final_kernel(at_ref, h0, g0, h1, g1, h2, g2, down_ref, up_ref):
    model = up_ref.shape[0]
    first = SLABS * h0.shape[1]
    cut = (down_ref.shape[0] - first) // h1.shape[1]

    def down0(row, value):
        down_ref[pl.ds(row, value.shape[0]), :] = value

    def down1(row, value):
        down_ref[pl.ds(first + row, value.shape[0]), :] = value

    def left(row, value):
        up_ref[pl.ds(row, value.shape[0]), :model] = value

    def right(row, value):
        up_ref[pl.ds(row, value.shape[0]), model:] = value

    each_slab(at_ref[1], h0, g0, 0, SLABS, down0)
    each_slab(at_ref[2], h1, g1, 0, cut, down1)
    each_slab(at_ref[2], h1, g1, cut, SLABS, left)
    each_slab(at_ref[3], h2, g2, 0, SLABS, right)


def attn_final_kernel(at_ref, h0, g0, h1, g1, h2, g2, qkv_ref, out_ref):
    width = qkv_ref.shape[2]
    cut = width // h1.shape[1]

    def two(row, value):
        qkv_ref[0, pl.ds(row, value.shape[0]), :] = value[:, :width]
        qkv_ref[1, pl.ds(row, value.shape[0]), :] = value[:, width:]

    def folded(row, value):
        qkv_ref[2, pl.ds(row, value.shape[0]), :] = value[:, :width]
        qkv_ref[2, pl.ds(width + row, value.shape[0]), :] = value[:, width:]

    def out1(row, value):
        out_ref[pl.ds(row, value.shape[0]), :] = value

    def out2(row, value):
        out_ref[pl.ds(PAIR + row, value.shape[0]), :] = value

    each_slab(at_ref[1], h0, g0, 0, SLABS, two)
    each_slab(at_ref[2], h1, g1, 0, cut, folded)
    each_slab(at_ref[2], h1, g1, cut, SLABS, out1)
    each_slab(at_ref[3], h2, g2, 0, SLABS, out2)


def input_grad_kernel(at_ref, grad_ref, w_ref, pre_ref, send_ref, own_ref):
    half = SEQ_LEN // 2
    own = pl.multiple_of(at_ref[0], half)
    other = half - own
    for start, ref in ((other, send_ref), (own, own_ref)):
        total = pre_ref[...] if ref is own_ref else None
        for k in range(3):
            value = dot(grad_ref[k, pl.ds(start, half), :], w_ref[k], NT)
            total = value if total is None else total + value
        ref[...] = total.astype(ref.dtype)


def swap(values):
    return lax.ppermute(values, "tensor", [(0, 1), (1, 0)])


ORDERS = ((0, 1, 2, 3), (1, 0, 2, 3), (2, 3, 0, 1))


def exchange(values, count, bit):
    return lax.ppermute(values, "dp", [(i, i ^ (1 << bit)) for i in range(count)])


def spots(index, count):
    if count != SLABS:
        return [jnp.int32(0)] * 3
    return [
        sum(((index >> bit) & 1) << (3 - s) for s, bit in enumerate(order)) for order in ORDERS
    ]


def halve_first(sends, count):
    return [exchange(send, count, ORDERS[k][0]) for k, send in enumerate(sends)]


def add_low(a, b):
    return (a.astype(F32) + b.astype(F32)).astype(BF16)


def halve_rest(keeps, gots, count):
    held = list(keeps)
    for s in range(1, 5):
        for k in range(3):
            half = held[k].shape[0] // 2
            if s == 4:
                held[k] = add_low(held[k], gots[k])
                continue
            send = add_low(held[k][half:], gots[k][half:])
            held[k] = add_low(held[k][:half], gots[k][:half])
            gots[k] = exchange(send, count, ORDERS[k][s])
    return held


def double(held, count):
    held = list(held)
    gots = [None] * 3
    for s in (3, 2, 1, 0):
        for k in range(3):
            if gots[k] is not None:
                held[k] = jnp.concatenate([held[k], gots[k]], axis=0)
            gots[k] = exchange(held[k], count, ORDERS[k][s])
    return held, gots


def sum_plain(keeps, sends):
    pairs = [
        lax.psum(jnp.concatenate([k, s], axis=0).astype(F32), "dp").astype(BF16)
        for k, s in zip(keeps, sends)
    ]
    half = SLABS // 2
    return [p[:half] for p in pairs], [p[half:] for p in pairs]


def sum_small(values):
    count = lax.axis_size("dp")
    for bit in range(count.bit_length() - 1):
        values = values + exchange(values, count, bit)
    return values


def per_device(
    tokens, lengths, w_qkv, b_qv, conv_pool, w_out, b_out, ln_gain, ln_bias,
    w_up, b_up, w_down, b_down, grad_output,
):
    member = lax.axis_index("tensor")
    index = lax.axis_index("dp")
    count = lax.axis_size("dp")
    token_count, model = tokens.shape
    assert token_count == SEQ_LEN and lengths.shape[0] == 1
    half = token_count // 2
    width = w_qkv.shape[2]
    units = w_up.shape[1]
    lane = lax.iota(jnp.int32, 4)
    at = jnp.where(lane == 0, member * half, 0)
    for k, spot in enumerate(spots(index, count)):
        at = jnp.where(lane == k + 1, spot, at)

    forward = attend_forward(at, tokens, lengths, w_qkv, b_qv, conv_pool, w_out)
    attended, out_send, out_own = forward[7:]
    saved = forward[:7]
    normed, normed_low, normed_hat, normed_scale = call(
        first_norm_kernel,
        "first_norm",
        [((half, model), F32), ((half, model), BF16), ((half, model), BF16), ((half, 1), F32)],
        (at, tokens, out_own, swap(out_send), b_out.reshape(1, model), ln_gain, ln_bias),
        in_specs=[scalars()] + [whole()] * 6,
    )
    normed_got = swap(normed_low)
    up_row = b_up.reshape(1, units)
    gated_own, slope_own, part = feed(
        normed_low, w_up, up_row, w_down, normed, b_down.reshape(1, model)
    )
    gated_other, slope_other, down_send = feed(normed_got, w_up, up_row, w_down)
    layer_output, grad_summed, summed_low, top_sums = call(
        second_norm_kernel,
        "second_norm",
        [((half, model), BF16), ((half, model), F32), ((half, model), BF16), ((8, model), F32)],
        (part, swap(down_send), ln_gain, ln_bias, grad_output),
    )
    summed_got = swap(summed_low)
    hidden_own, bias_own, up_own = back(summed_low, slope_own, w_down, w_up, grad_summed)

    rows0, rows1, rows2 = 80 * SLABS, 64 * SLABS, 48 * SLABS
    keep0, send0 = call(
        down_grad_kernel,
        "down_grad",
        slab_outs(rows0, model),
        (at, gated_own, gated_other, summed_low, summed_got),
        in_specs=[scalars()] + [whole()] * 4,
        scratch=[pltpu.VMEM((rows0, model), BF16)],
        cost=(2_000_000_000, 7_000_000),
    )
    hidden_other, bias_other, up_send = back(summed_got, slope_other, w_down, w_up)
    last = pl.BlockSpec((half, UNITS), lambda i: (0, rows0 // UNITS))
    keep1, send1, keep2, send2 = call(
        up_grad_kernel,
        "up_grad",
        slab_outs(rows1, model) + slab_outs(rows2, model),
        (
            at, gated_own, gated_other, summed_low, summed_got,
            normed_low, normed_got, hidden_own, hidden_other,
        ),
        grid=(1,),
        in_specs=[scalars(), last, last] + [whole()] * 6,
        scratch=[pltpu.VMEM((rows1, model), BF16), pltpu.VMEM((rows2, model), BF16)],
        cost=(3_000_000_000, 9_000_000),
    )
    feed_keeps, feed_sends = [keep0, keep1, keep2], [send0, send1, send2]
    feed_gots = halve_first(feed_sends, count) if count == SLABS else None

    grad_pre, pre_low, first_sums = call(
        first_back_kernel,
        "first_back",
        [((half, model), F32), ((half, model), BF16), ((8, model), F32)],
        (up_own, swap(up_send), normed_hat, normed_scale, ln_gain),
    )
    pre_got = swap(pre_low)
    grad_qkv_low, grad_conv, grad_qv_bias = attend_backward(
        at, saved, pre_low, pre_got, w_out, conv_pool
    )
    if count == SLABS:
        feed_gots, grad_qkv_low = lax.optimization_barrier((feed_gots, grad_qkv_low))
    attn = call(
        attn_grad_kernel,
        "attn_grad",
        slab_outs(768, model) + slab_outs(512, model) + slab_outs(256, model),
        (at, tokens, grad_qkv_low, attended, pre_low, pre_got),
        in_specs=[scalars()] + [whole()] * 5,
        scratch=[pltpu.VMEM((rows, model), BF16) for rows in (768, 512, 256)],
        cost=(3_000_000_000, 9_000_000),
    )
    attn_keeps, attn_sends = attn[0::2], attn[1::2]
    input_send, input_own = call(
        input_grad_kernel,
        "input_grad",
        [((half, model), BF16), ((half, model), F32)],
        (at, grad_qkv_low, w_qkv, grad_pre),
        in_specs=[scalars()] + [whole()] * 3,
    )
    grad_input = input_own + swap(input_send).astype(F32)
    if count == SLABS:
        attn_gots = halve_first(attn_sends, count)
        feed_held, feed_gots = double(halve_rest(feed_keeps, feed_gots, count), count)
        attn_held, attn_gots = double(halve_rest(attn_keeps, attn_gots, count), count)
    else:
        feed_held, feed_gots = sum_plain(feed_keeps, feed_sends)
        attn_held, attn_gots = sum_plain(attn_keeps, attn_sends)
    woven = lambda held, gots: [a for pair in zip(held, gots) for a in pair]
    grad_down, grad_up = call(
        feed_final_kernel,
        "feed_final",
        [((units, model), F32), ((model, units), F32)],
        (at, *woven(feed_held, feed_gots)),
        in_specs=[scalars()] + [whole()] * 6,
    )
    grad_qkv, grad_out = call(
        attn_final_kernel,
        "attn_final",
        [((3, model, width), F32), ((width, model), F32)],
        (at, *woven(attn_held, attn_gots)),
        in_specs=[scalars()] + [whole()] * 6,
    )

    norm_rows = jnp.concatenate([first_sums[0:3], top_sums[0:3]], axis=0)
    norm_rows = norm_rows + swap(norm_rows)
    small = jnp.concatenate(
        [
            norm_rows.reshape(-1, width),
            grad_qv_bias,
            grad_conv.reshape(-1, width),
            (bias_own + bias_other).reshape(-1, width),
        ],
        axis=0,
    )
    small = sum_small(jnp.pad(small, ((0, -small.shape[0] % 8), (0, 0))))
    norm_rows = small[: 6 * model // width].reshape(6, model)
    rest = small[6 * model // width :]
    return (
        layer_output,
        grad_input,
        grad_qkv,
        rest[0:2],
        rest[2 : 2 + 2 * STRIDE].reshape(2, STRIDE, width),
        grad_out,
        norm_rows[2],
        jnp.stack([norm_rows[0], norm_rows[3]]),
        jnp.stack([norm_rows[1], norm_rows[4]]),
        grad_up,
        rest[2 + 2 * STRIDE : 2 + 2 * STRIDE + units // width].reshape(units),
        grad_down,
        norm_rows[5],
    )


def solution(mesh):
    placed = (
        P("dp", None),
        P("dp", None),
        P(None, None, "tensor"),
        P(None, "tensor"),
        P(None, None, "tensor"),
        P("tensor", None),
        P(),
        P(),
        P(),
        P(None, "tensor"),
        P("tensor"),
        P("tensor", None),
        P(),
        P(("dp", "tensor"), None),
    )
    return jax.shard_map(
        per_device,
        mesh=mesh,
        in_specs=placed,
        out_specs=(
            P(("dp", "tensor"), None),
            P(("dp", "tensor"), None),
            P(None, None, "tensor"),
            P(None, "tensor"),
            P(None, None, "tensor"),
            P("tensor", None),
            P(),
            P(),
            P(),
            P(None, "tensor"),
            P("tensor"),
            P("tensor", None),
            P(),
        ),
        check_vma=False,
    )
```
